32 devices in a mesh: seq: 2 (over core), depth: 2 (over x), vocab: 8 (over z, y).
Axes of the slice: x: 2, y: 2, z: 4, core: 2. Of those that a mesh axis runs over, the one named last changes fastest.
Arguments:
- hidden: bfloat16 [2, 128, 7168], P('depth', ('seq', 'vocab')), may hold values from -24 to 24
- embedding: bfloat16 [16160, 7168], P(('seq', 'vocab')), may hold values from -1 to 1
- targets: int32 [2, 128], P('depth', ('seq', 'vocab')), may hold values from 0 to 16159
- mask: int32 [2, 128], P('depth', ('seq', 'vocab')), may hold values 0 or 1
Outputs:
- nll: float32 [2, 128], P('depth', ('seq', 'vocab'))
- loss: float32 [], replicated
- grad_norm: float32 [], replicated
The draws below stay inside these ranges and needn't reach their ends.
All inputs are finite; a program needn't handle non-finite values. No bound on the sum of `mask` on one device may be relied on, other than what follows from the above.
Results may differ from the reference program's by a relative error of at most 0.0023.
Values may be sent and summed in bfloat16 or wider, within the bound.
No kernel may reach another device: no remote copies, remote signals or barrier semaphores. Data moves between devices by JAX's collectives and lax.ppermute only.
A program may use at most 128 MiB of HBM per device.

```python
import math
import jax
import jax.numpy as jnp
from jax import lax

D = 7168
VOC_DEV = 1010
TOKENS = 128
VOCAB = 16160


def shared_tables(key):
    base = jax.random.fold_in(key, 7)
    keys = jax.random.split(base, 10)
    table = jnp.clip(jax.random.normal(keys[0], (VOCAB, D), jnp.float32) * (3.0 / math.sqrt(D)), -1.0, 1.0)
    noise = jax.random.normal(keys[1], (2, TOKENS, D), jnp.float32)
    states = jnp.stack([noise[0], 0.9 * noise[0] + 0.44 * noise[1]])
    channels = jax.random.randint(keys[7], (8,), 0, D)
    sizes = jax.random.uniform(keys[8], (8,), jnp.float32, 6.0, 14.0)
    signs = jnp.where(jax.random.bernoulli(keys[9], 0.5, (8,)), jnp.float32(1.0), jnp.float32(-1.0))
    columns = jnp.arange(D, dtype=jnp.int32)
    shared = jnp.sum(jnp.where(channels[:, None] == columns[None, :], (sizes * signs)[:, None], jnp.float32(0.0)), axis=0)
    states = states + shared[None, None, :]
    return (table, jnp.clip(states, -24.0, 24.0))


def draw_hidden(key, part):
    table, states = shared_tables(key)
    return states.astype(jnp.bfloat16)


def draw_embedding(key, part):
    table, states = shared_tables(key)
    return table.astype(jnp.bfloat16)


def draw_targets(key, part):
    keys = jax.random.split(jax.random.fold_in(key, 11), 5)
    common = jax.random.randint(keys[0], (64,), 0, VOCAB)
    first = jax.random.randint(keys[1], (TOKENS + 1,), 0, 64)
    second = jax.random.randint(keys[2], (TOKENS + 1,), 0, 64)
    frequent = common[jnp.minimum(first, second)]
    spread = jax.random.randint(keys[3], (TOKENS + 1,), 0, VOCAB)
    select = jax.random.randint(keys[4], (TOKENS + 1,), 0, 4)
    sequence = jnp.where(select == 0, spread, frequent).astype(jnp.int32)
    return jnp.stack([sequence[:TOKENS], sequence[1:]]).astype(jnp.int32)


def with_ends(entries, own_key, smallest, high):
    extent = entries.shape
    index_at = [jax.random.randint(jax.random.fold_in(own_key, axis), (), 0, extent[axis]) for axis in range(len(extent))]
    entries = entries.at[tuple(index_at)].set(smallest)
    longest = extent.index(max(extent))
    index_at[longest] = (index_at[longest] + 1) % extent[longest]
    return entries.at[tuple(index_at)].set(high)


def setup_inputs(seed: int = 0) -> dict:
    streams_of = jax.random.split(jax.random.key(seed), 5)
    hidden = draw_hidden(jax.random.fold_in(streams_of[4], 71), 0)
    embedding = draw_embedding(jax.random.fold_in(streams_of[4], 71), 0)
    targets = draw_targets(jax.random.fold_in(streams_of[4], 71), 0)
    mask = with_ends((jax.random.randint(streams_of[3], (2, TOKENS), 0, 4) < 3).astype(jnp.int32), jax.random.fold_in(streams_of[3], 1), 0, 1)
    return {"hidden": hidden, "embedding": embedding, "targets": targets, "mask": mask}


def reference(hidden, embedding, targets, mask):
    ids = jnp.arange(VOCAB, dtype=jnp.int32)
    head_weights = (1.0, 0.3)
    loss = jnp.zeros((), jnp.float32)
    nll_rows = []
    grads = []
    for head in range(2):
        states = hidden[head]
        logits = lax.dot_general(states, embedding, (((1,), (1,)), ((), ())), preferred_element_type=jnp.float32)
        peak = lax.optimization_barrier(jnp.max(logits, axis=1))
        total = lax.optimization_barrier(jnp.sum(jnp.exp(logits - peak[:, None]), axis=1))
        lse = peak + jnp.log(total)
        onehot = targets[head][:, None] == ids[None, :]
        chosen = lax.optimization_barrier(jnp.sum(jnp.where(onehot, logits, jnp.zeros((), jnp.float32)), axis=1))
        nll = lse - chosen
        live = mask[head].astype(jnp.float32)
        coef = head_weights[head] / jnp.maximum(jnp.sum(live), jnp.float32(1.0))
        loss = loss + coef * jnp.sum(live * nll)
        grad_logits = (coef * live[:, None] * (jnp.exp(logits - lse[:, None]) - onehot.astype(jnp.float32))).astype(jnp.bfloat16)
        nll_rows.append(nll)
        grads.append(grad_logits)

    def block_square(index):
        start = (index * VOC_DEV).astype(jnp.int32)
        summed = jnp.zeros((VOC_DEV, D), jnp.float32)
        for head in range(2):
            piece = lax.dynamic_slice_in_dim(grads[head], start, VOC_DEV, 1)
            part = jnp.dot(piece.T, hidden[head], preferred_element_type=jnp.float32).astype(jnp.bfloat16)
            part = lax.optimization_barrier(part)
            summed = summed + part.astype(jnp.float32)
        return jnp.sum(summed * summed)
    squares = lax.map(block_square, jnp.arange(VOCAB // VOC_DEV, dtype=jnp.int32))
    grad_norm = jnp.sqrt(jnp.sum(squares))
    return (jnp.stack(nll_rows), loss, grad_norm)
```

```python
import functools

import jax
import jax.numpy as jnp
from jax import lax
from jax.experimental import pallas as pl
from jax.experimental.pallas import tpu as pltpu
from jax.sharding import PartitionSpec as P

GROUP = ("seq", "vocab")
EVERY = ("seq", "depth", "vocab")
SCALE = 2.0**40
WEIGHTS = (1.0, 0.3)
HIGH = lax.Precision.HIGHEST


def exchange_masks(size):
    bits = size.bit_length() - 1
    assert size == 2**bits
    return [2**bit ^ (2 ** (bit - 1) if bit >= 2 else 0) for bit in range(bits)]


def round_pairs(masks, turn, cores, size):
    pairs = []
    for core in range(cores):
        mask = masks[(turn + core) % len(masks)]
        pairs += [(core * size + at, core * size + (at ^ mask)) for at in range(size)]
    return pairs


def swapped(value, axis):
    return lax.ppermute(value, axis, [(0, 1), (1, 0)])


def token_order(masks, size, count):
    total = 2 * size * count
    row = lax.broadcasted_iota(jnp.int32, (total, 1), 0)
    core = lax.axis_index("seq") ^ (row // (size * count))
    slot = (row // count) % size
    at = jnp.broadcast_to(lax.axis_index("vocab"), row.shape)
    for turn in range(len(masks)):
        bit = (slot >> turn) & 1
        first, second = masks[turn % len(masks)], masks[(turn + 1) % len(masks)]
        at = at ^ (bit * jnp.where(core == 0, first, second))
    return (core * size + at) * count + row % count


def rows_dot(a, b, dims, precision=None):
    return lax.dot_general(
        a, b, ((dims[:1], dims[1:]), ((), ())), precision=precision, preferred_element_type=jnp.float32
    )


def logits_kernel(
    width, half, steps, own_ref, twin_ref, side_ref, table_ref, perm_ref, meta_ref,
    logits_ref, send_ref, gram_ref, pack_ref,
):
    step = pl.program_id(0)

    @pl.when(step == 0)
    def _():
        logits_ref[...] = jnp.zeros_like(logits_ref)
        gram_ref[...] = jnp.zeros_like(gram_ref)
        pack_ref[...] = jnp.zeros_like(pack_ref)

    states = jnp.concatenate([own_ref[...], twin_ref[...]], axis=0)
    logits_ref[:width, :] += rows_dot(table_ref[...], states, (1, 1))
    gram_ref[...] += rows_dot(states, states, (1, 1))
    pack_ref[8:, :] += rows_dot(side_ref[...], states, (1, 1))

    @pl.when(step == steps - 1)
    def _():
        depth = lax.axis_index("depth")
        logits = logits_ref[...]
        valid = lax.broadcasted_iota(jnp.int32, logits.shape, 0) < width
        peak = jnp.max(jnp.where(valid, logits, -jnp.inf), axis=0, keepdims=True)
        total = jnp.sum(jnp.where(valid, jnp.exp(logits - peak), 0.0), axis=0, keepdims=True)
        send_ref[...] = logits_ref[pl.ds(pl.multiple_of((1 - depth) * half, 8), half), :]
        rows = lax.broadcasted_iota(jnp.int32, (8, peak.shape[1]), 0)
        stats = jnp.where(rows == 0, peak, jnp.where(rows == 1, total, 0.0))
        both = jnp.concatenate([stats, pack_ref[8:, :]], axis=0)
        both = rows_dot(both, perm_ref[...], (1, 0), HIGH)
        pack_ref[...] = both + meta_ref[...]


def gradient_kernel(
    width, half, sizes, logits_ref, peer_ref, recv_ref, perm_ref, gram_ref, base_ref, pack_ref, keep_ref
):
    cores, vocabs, count = sizes
    depth = lax.axis_index("depth")
    tokens = perm_ref.shape[0]
    peers = [(core, at) for core in range(cores) for at in range(vocabs)]

    def head(which):
        parts = [recv_ref[core, which, at, 0:8, :] for core, at in peers]
        peak = functools.reduce(jnp.maximum, parts)[0:1, :]
        total = sum(part[1:2, :] * jnp.exp(part[0:1, :] - peak) for part in parts)
        meta = functools.reduce(jnp.add, parts)
        live = meta[3:4, :]
        weight = jnp.where(which == 0, jnp.float32(WEIGHTS[0]), jnp.float32(WEIGHTS[1]))
        scale = live * (weight / jnp.maximum(jnp.sum(live), 1.0))
        return peak + jnp.log(total), meta[2:3, :], scale

    lse, target, scale = head(depth)
    lse_peer, target_peer, scale_peer = head(1 - depth)
    rows = lax.broadcasted_iota(jnp.int32, (8, tokens), 0)
    vectors = jnp.zeros((8, tokens), jnp.float32)
    for at, vector in enumerate((lse, target, scale, lse_peer, target_peer, scale_peer)):
        vectors = jnp.where(rows == at, vector, vectors)
    keep_ref[...] = vectors
    vectors = rows_dot(vectors, perm_ref[...], (1, 1), HIGH)

    base = base_ref[0]
    shift = pl.multiple_of(depth * half, 8)

    def gradient(logits, at, first):
        row = lax.broadcasted_iota(jnp.int32, logits.shape, 0) + first
        hit = (row + base) == vectors[at + 1 : at + 2, :].astype(jnp.int32)
        soft = jnp.exp(logits - vectors[at : at + 1, :]) - jnp.where(hit, 1.0, 0.0)
        grad = (vectors[at + 2 : at + 3, :] * SCALE) * soft
        return hit, jnp.where(row < width, grad, 0.0).astype(jnp.bfloat16)

    logits = logits_ref[...]
    hit, grad = gradient(logits, 0, 0)
    chosen = jnp.sum(jnp.where(hit, logits, 0.0), axis=0, keepdims=True)
    _, mine = gradient(logits_ref[pl.ds(shift, half), :], 0, shift)
    _, grad_peer = gradient(peer_ref[...], 3, shift)
    inner = rows_dot(grad, grad, (0, 0))
    cross = rows_dot(grad_peer, mine, (0, 0))
    cross = rows_dot(perm_ref[...], cross, (0, 0), HIGH)
    cross = rows_dot(cross, perm_ref[...], (1, 0), HIGH)
    sides = jnp.concatenate([recv_ref[core, depth, at, 8 : 8 + count, :] for core, at in peers], axis=0)
    square = jnp.sum(inner * gram_ref[...] + 2.0 * cross * sides, axis=0, keepdims=True)
    chosen = rows_dot(jnp.broadcast_to(chosen, (8, tokens)), perm_ref[...], (1, 0), HIGH)
    pack_ref[...] = jnp.where(rows == depth, chosen, jnp.where(rows == 2, square, 0.0))


def final_kernel(sizes, recv_ref, keep_ref, nll_ref, loss_ref, norm_ref):
    count = sizes[2]
    depth = lax.axis_index("depth")
    total = jnp.sum(recv_ref[...], axis=0)
    keep = keep_ref[...]
    own = jnp.where(depth == 0, total[0:1, :], total[1:2, :])
    peer = jnp.where(depth == 0, total[1:2, :], total[0:1, :])
    nll = keep[0:1, :] - own
    loss_ref[0, 0] = jnp.sum(keep[2:3, :] * nll) + jnp.sum(keep[5:6, :] * (keep[3:4, :] - peer))
    square = jnp.maximum(jnp.sum(total[2:3, :]), 0.0)
    norm_ref[0, 0] = square
    nll_ref[...] = nll


def everyone(value, size):
    spread = jnp.broadcast_to(value[None], (size,) + value.shape)
    return lax.all_to_all(spread, EVERY, 0, 0, tiled=True)


def local(hidden, embedding, targets, mask):
    cores, depths, vocabs = (lax.axis_size(axis) for axis in EVERY)
    assert cores == 2 and depths == 2
    count, dim = hidden.shape[1:]
    width = embedding.shape[0]
    half = -(-width // 16) * 8
    tokens = cores * vocabs * count
    masks = exchange_masks(vocabs)
    place = lax.axis_index(GROUP)
    sizes = (cores, vocabs, count)

    own = hidden[0]
    side = swapped(own, "depth")
    for turn in range(len(masks)):
        own = jnp.concatenate([own, lax.ppermute(own, GROUP, round_pairs(masks, turn, cores, vocabs))], axis=0)
    twin = swapped(own, "seq")

    order = token_order(masks, vocabs, count)
    column = lax.broadcasted_iota(jnp.int32, (tokens, tokens), 1)
    perm = (order == column).astype(jnp.float32)
    lane = lax.broadcasted_iota(jnp.int32, (count, tokens), 1)
    spot = (lane == place * count + lax.broadcasted_iota(jnp.int32, (count, tokens), 0)).astype(jnp.float32)
    placed = [jnp.sum(spot * value[0][:, None].astype(jnp.float32), axis=0) for value in (targets, mask)]
    line = lax.broadcasted_iota(jnp.int32, (8 + count, tokens), 0)
    meta = jnp.where(line == 2, placed[0][None, :], jnp.where(line == 3, placed[1][None, :], 0.0))

    chunk = 512 if dim % 512 == 0 else 128
    steps = dim // chunk
    still = lambda step: (0, 0)
    moving = lambda step: (0, step)
    f32 = jnp.float32
    logits, send, gram, pack = pl.pallas_call(
        functools.partial(logits_kernel, width, half, steps),
        grid=(steps,),
        in_specs=[
            pl.BlockSpec((tokens // 2, chunk), moving),
            pl.BlockSpec((tokens // 2, chunk), moving),
            pl.BlockSpec((count, chunk), moving),
            pl.BlockSpec((width, chunk), moving),
            pl.BlockSpec((tokens, tokens), still),
            pl.BlockSpec((8 + count, tokens), still),
        ],
        out_specs=[
            pl.BlockSpec((2 * half, tokens), still),
            pl.BlockSpec((half, tokens), still),
            pl.BlockSpec((tokens, tokens), still),
            pl.BlockSpec((8 + count, tokens), still),
        ],
        out_shape=[
            jax.ShapeDtypeStruct((2 * half, tokens), f32),
            jax.ShapeDtypeStruct((half, tokens), f32),
            jax.ShapeDtypeStruct((tokens, tokens), f32),
            jax.ShapeDtypeStruct((8 + count, tokens), f32),
        ],
        name="logits",
    )(own, twin, side, embedding, perm, meta)

    peer = swapped(send, "depth")
    recv = everyone(pack, cores * depths * vocabs)
    recv = recv.reshape(cores, depths, vocabs, 8 + count, tokens)
    base = (place * width).astype(jnp.int32).reshape(1)

    vmem = pl.BlockSpec(memory_space=pltpu.VMEM)
    smem = pl.BlockSpec(memory_space=pltpu.SMEM)
    pack, keep = pl.pallas_call(
        functools.partial(gradient_kernel, width, half, sizes),
        in_specs=[vmem] * 5 + [smem],
        out_specs=[vmem] * 2,
        out_shape=[jax.ShapeDtypeStruct((8, tokens), f32)] * 2,
        name="gradient",
    )(logits, peer, recv, perm, gram, base)

    recv = everyone(pack, cores * depths * vocabs)
    nll, loss, square = pl.pallas_call(
        functools.partial(final_kernel, sizes),
        in_specs=[vmem] * 2,
        out_specs=[vmem, smem, smem],
        out_shape=[
            jax.ShapeDtypeStruct((1, tokens), f32),
            jax.ShapeDtypeStruct((1, 1), f32),
            jax.ShapeDtypeStruct((1, 1), f32),
        ],
        name="final",
    )(recv, keep)
    norm = jnp.sqrt(square[0, 0]) * jnp.float32(1.0 / SCALE)
    return (lax.dynamic_slice_in_dim(nll, place * count, count, 1), loss[0, 0], norm)


def solution(mesh):
    placed = (
        P("depth", GROUP, None),
        P(GROUP, None),
        P("depth", GROUP),
        P("depth", GROUP),
    )
    return jax.shard_map(
        local,
        mesh=mesh,
        in_specs=placed,
        out_specs=(P("depth", GROUP), P(), P()),
        check_vma=False,
    )
```

```python
import functools

import jax
import jax.numpy as jnp
from jax import lax
from jax.experimental import pallas as pl
from jax.experimental.pallas import tpu as pltpu
from jax.sharding import PartitionSpec as P


GROUP = ("seq", "vocab")
EVERY = ("seq", "depth", "vocab")
SCALE = 2.0**40
WEIGHTS = (1.0, 0.3)
HIGH = lax.Precision.HIGHEST
LIMIT = 24 * 2**20
PIECES = 4
VMEM = pl.BlockSpec(memory_space=pltpu.VMEM)


def exchange_masks(size):
    bits = size.bit_length() - 1
    assert size == 2**bits and bits >= 2
    return [2**bit for bit in range(bits - 1, 1, -1)] + [1, 2]


def moved(value, axis, mask):
    return lax.ppermute(value, axis, [(at, at ^ mask) for at in range(lax.axis_size(axis))])


def token_order(masks, size, count):
    total = 2 * size * count
    row = lax.broadcasted_iota(jnp.int32, (total, 1), 0)
    core = lax.axis_index("seq") ^ (row // (size * count))
    slot = (row // count) % size
    at = jnp.broadcast_to(lax.axis_index("vocab"), row.shape)
    for turn, mask in enumerate(masks):
        at = at ^ (((slot >> turn) & 1) * mask)
    return (core * size + at) * count + row % count


def rows_dot(a, b, dims, precision=None):
    return lax.dot_general(
        a, b, ((dims[:1], dims[1:]), ((), ())), precision=precision, preferred_element_type=jnp.float32
    )


def fetch_kernel(start, table_ref, copy_ref, sems):
    pieces, columns = sems.shape[0], copy_ref.shape[1]
    chunk = columns // pieces
    copies = [
        pltpu.make_async_copy(
            table_ref.at[:, pl.ds(start + at * chunk, chunk)], copy_ref.at[:, pl.ds(at * chunk, chunk)], sems.at[at]
        )
        for at in range(pieces)
    ]
    for copy in copies:
        copy.start()
    for copy in copies:
        copy.wait()


def early_kernel(own_ref, twin_ref, table_ref, logits_ref):
    states = jnp.concatenate([own_ref[...], twin_ref[...]], axis=0)
    logits_ref[: table_ref.shape[0], :] = rows_dot(table_ref[...], states, (1, 1))


def folded(block, which):
    tokens = block.shape[1]
    turned = pltpu.roll(block, tokens // 2, 1)
    first = jnp.where(which == 0, block, turned)
    second = jnp.where(which == 0, turned, block)
    lane = lax.broadcasted_iota(jnp.int32, (4, tokens), 1)
    return [
        jnp.where(lane < tokens // 2, first[at : at + 4], second[at + 4 : at + 8])
        for at in range(0, block.shape[0], 8)
    ]


def logits_kernel(
    start, width, half, size, own_ref, twin_ref, table_ref, early_ref, own_early_ref, twin_early_ref, side_ref,
    perm_ref, meta_ref, logits_ref, send_ref, gram_ref, pack_ref,
):
    early = jnp.concatenate([own_early_ref[...], twin_early_ref[...]], axis=0)
    late = jnp.concatenate([own_ref[...], twin_ref[...]], axis=0)
    gram_ref[...] = rows_dot(early, early, (1, 1)) + rows_dot(late, late, (1, 1))
    cross = rows_dot(side_ref[:, :start], early, (1, 1)) + rows_dot(side_ref[:, start:], late, (1, 1))
    logits = rows_dot(table_ref[...], late, (1, 1)) + early_ref[:width, :]
    logits_ref[:width, :] = logits
    logits_ref[width:, :] = jnp.zeros((2 * half - width, logits.shape[1]), jnp.float32)
    depth = lax.axis_index("depth")
    send_ref[...] = logits_ref[pl.ds(pl.multiple_of((1 - depth) * half, 8), half), :]
    peak = jnp.max(logits, axis=0, keepdims=True)
    total = jnp.sum(jnp.exp(logits - peak), axis=0, keepdims=True)
    rows = lax.broadcasted_iota(jnp.int32, cross.shape, 0)
    stats = jnp.where(rows == 0, peak, jnp.where(rows == 1, total, 0.0))
    stats = rows_dot(stats, perm_ref[...], (1, 0), HIGH) + meta_ref[...]
    cross = rows_dot(cross, perm_ref[...], (1, 0), HIGH)
    parts = [stats[:4]] + folded(cross, lax.axis_index("seq") ^ depth)
    for peer in range(size):
        for at, part in enumerate(parts):
            pack_ref[peer * len(parts) + at] = part


def gradient_kernel(
    width, half, sizes, logits_ref, peer_ref, recv_ref, perm_ref, gram_ref, base_ref, pack_ref, keep_ref
):
    cores, vocabs, count = sizes
    depth = lax.axis_index("depth")
    tokens = perm_ref.shape[0]
    stride = 1 + count // 8
    peers = [(core, at) for core in range(cores) for at in range(vocabs)]

    def first(core, which, at):
        return ((core * 2 + which) * vocabs + at) * stride

    def head(which):
        parts = [recv_ref[first(core, which, at)] for core, at in peers]
        peak = functools.reduce(jnp.maximum, parts)[0:1, :]
        total = sum(part[1:2, :] * jnp.exp(part[0:1, :] - peak) for part in parts)
        meta = functools.reduce(jnp.add, parts)
        live = meta[3:4, :]
        weight = jnp.where(which == 0, jnp.float32(WEIGHTS[0]), jnp.float32(WEIGHTS[1]))
        scale = live * (weight / jnp.maximum(jnp.sum(live), 1.0))
        return peak + jnp.log(total), meta[2:3, :], scale

    lse, target, scale = head(depth)
    lse_peer, target_peer, scale_peer = head(1 - depth)
    rows = lax.broadcasted_iota(jnp.int32, (8, tokens), 0)
    vectors = jnp.zeros((8, tokens), jnp.float32)
    for at, vector in enumerate((lse, target, scale, lse_peer, target_peer, scale_peer)):
        vectors = jnp.where(rows == at, vector, vectors)
    keep_ref[...] = vectors
    vectors = rows_dot(vectors, perm_ref[...], (1, 1), HIGH)

    base = base_ref[0]
    shift = pl.multiple_of(depth * half, 8)

    def gradient(logits, at, start):
        row = lax.broadcasted_iota(jnp.int32, logits.shape, 0) + start
        hit = (row + base) == vectors[at + 1 : at + 2, :].astype(jnp.int32)
        soft = jnp.exp(logits - vectors[at : at + 1, :]) - jnp.where(hit, 1.0, 0.0)
        grad = (vectors[at + 2 : at + 3, :] * SCALE) * soft
        return hit & (row < width), jnp.where(row < width, grad, 0.0).astype(jnp.bfloat16)

    logits = logits_ref[...]
    hit, grad = gradient(logits, 0, 0)
    chosen = jnp.sum(jnp.where(hit, logits, 0.0), axis=0, keepdims=True)
    _, mine = gradient(logits_ref[pl.ds(shift, half), :], 0, shift)
    _, grad_peer = gradient(peer_ref[...], 3, shift)
    inner = rows_dot(grad, grad, (0, 0))
    cross = rows_dot(grad_peer, mine, (0, 0))
    cross = rows_dot(perm_ref[...], cross, (0, 0), HIGH)
    cross = rows_dot(cross, perm_ref[...], (1, 0), HIGH)
    square = inner * gram_ref[...]
    flat = jnp.transpose(cross)
    lines = []
    for core in range(cores):
        for matrix, which in ((cross, depth), (flat, 1 - depth)):
            start = core * vocabs * count
            blocks = folded(matrix[start : start + vocabs * count], which ^ core)
            for at in range(vocabs):
                for part in range(count // 8):
                    tile = recv_ref[first(core, which, at) + 1 + part]
                    lines.append(blocks[at * (count // 8) + part] * tile)
    square = jnp.sum(square, axis=0, keepdims=True) + 2.0 * jnp.sum(sum(lines), axis=0, keepdims=True)
    chosen = rows_dot(jnp.broadcast_to(chosen, (8, tokens)), perm_ref[...], (1, 0), HIGH)
    pack = jnp.where(rows == depth, chosen, jnp.where(rows == 2, square, 0.0))[:4]
    for peer in range(2 * len(peers)):
        pack_ref[peer] = pack


def final_kernel(sizes, recv_ref, keep_ref, nll_ref, loss_ref, norm_ref):
    _, vocabs, count = sizes
    depth = lax.axis_index("depth")
    total = jnp.sum(recv_ref[...], axis=0)
    keep = keep_ref[...]
    own = jnp.where(depth == 0, total[0:1, :], total[1:2, :])
    peer = jnp.where(depth == 0, total[1:2, :], total[0:1, :])
    nll = keep[0:1, :] - own
    parts = keep[2:3, :] * nll + keep[5:6, :] * (keep[3:4, :] - peer)
    loss_ref[...] = jnp.sum(parts, axis=1, keepdims=True)
    square = jnp.maximum(jnp.sum(total[2:3, :], axis=1, keepdims=True), 0.0)
    norm_ref[...] = jnp.sqrt(square) * (1.0 / SCALE)
    tokens = nll.shape[1]
    place = lax.axis_index("seq") * vocabs + lax.axis_index("vocab")
    turned = pltpu.roll(jnp.broadcast_to(nll, (8, tokens)), tokens - place * count, 1)
    nll_ref[...] = turned[:1, :count]


def program(hidden, embedding, targets, mask):
    cores, depths, vocabs = (lax.axis_size(axis) for axis in EVERY)
    count, dim = hidden.shape[1:]
    assert cores == 2 and depths == 2 and count % 8 == 0 and dim % (256 * PIECES) == 0
    width = embedding.shape[0]
    half = -(-width // 16) * 8
    tokens = cores * vocabs * count
    size = cores * depths * vocabs
    masks = exchange_masks(vocabs)
    place = lax.axis_index(GROUP)
    sizes = (cores, vocabs, count)
    f32 = jnp.float32
    split = dim // 2

    own = hidden[0]
    left, right = own[:, :split], own[:, split:]
    for mask_far in masks[:-2]:
        left = jnp.concatenate([left, moved(left, "vocab", mask_far)], axis=0)
        right = jnp.concatenate([right, moved(right, "vocab", mask_far)], axis=0)
    rows = left.shape[0]
    left = jnp.concatenate([left, moved(left, "vocab", masks[-2])], axis=0)
    near = moved(right, "vocab", masks[-1])
    right = jnp.concatenate([right, near], axis=0)
    left = jnp.concatenate([left, moved(left, "vocab", masks[-1])], axis=0)
    last = moved(right, "vocab", masks[-2])
    right = jnp.concatenate([right[:rows], last[:rows], near, last[rows:]], axis=0)
    left, own = lax.optimization_barrier((left, own))
    left_twin = moved(left, "seq", 1)
    side = moved(own, "depth", 1)
    right_twin = moved(right, "seq", 1)

    order = token_order(masks, vocabs, count)
    column = lax.broadcasted_iota(jnp.int32, (tokens, tokens), 1)
    perm = (order == column).astype(f32)
    lane = lax.broadcasted_iota(jnp.int32, (count, tokens), 1)
    spot = (lane == place * count + lax.broadcasted_iota(jnp.int32, (count, tokens), 0)).astype(f32)
    placed = [jnp.sum(spot * value[0][:, None].astype(f32), axis=0) for value in (targets, mask)]
    line = lax.broadcasted_iota(jnp.int32, (count, tokens), 0)
    meta = jnp.where(line == 2, placed[0][None, :], jnp.where(line == 3, placed[1][None, :], 0.0))

    shape = lambda *dims: jax.ShapeDtypeStruct(dims, f32)
    params = pltpu.CompilerParams(vmem_limit_bytes=LIMIT)
    tables = []
    for start in (0, split):
        tables.append(
            pl.pallas_call(
                functools.partial(fetch_kernel, start),
                in_specs=[pl.BlockSpec(memory_space=pltpu.HBM)],
                out_specs=VMEM,
                out_shape=pltpu.VMEM((width, split), embedding.dtype),
                scratch_shapes=[pltpu.SemaphoreType.DMA((PIECES,))],
                compiler_params=pltpu.CompilerParams(vmem_limit_bytes=46 * 2**20),
                cost_estimate=pl.CostEstimate(flops=0, transcendentals=0, bytes_accessed=4 * width * split),
            )(embedding)
        )
    tables = [pltpu.with_memory_space_constraint(table, pltpu.VMEM) for table in tables]
    early = pl.pallas_call(
        early_kernel,
        in_specs=[VMEM] * 3,
        out_specs=VMEM,
        out_shape=shape(2 * half, tokens),
        compiler_params=params,
        name="early",
    )(left, left_twin, tables[0])
    logits, send, gram, pack = pl.pallas_call(
        functools.partial(logits_kernel, split, width, half, size),
        in_specs=[VMEM] * 9,
        out_specs=[VMEM] * 4,
        out_shape=[
            shape(2 * half, tokens),
            shape(half, tokens),
            shape(tokens, tokens),
            shape(size * (1 + count // 8), 4, tokens),
        ],
        compiler_params=params,
        name="logits",
    )(right, right_twin, tables[1], early, left, left_twin, side, perm, meta)

    peer = moved(send, "depth", 1)
    recv = lax.all_to_all(pack, EVERY, 0, 0, tiled=True)
    base = (place * width).astype(jnp.int32).reshape(1)
    pack, keep = pl.pallas_call(
        functools.partial(gradient_kernel, width, half, sizes),
        in_specs=[VMEM] * 5 + [pl.BlockSpec(memory_space=pltpu.SMEM)],
        out_specs=[VMEM] * 2,
        out_shape=[shape(size, 4, tokens), shape(8, tokens)],
        compiler_params=params,
        name="gradient",
    )(logits, peer, recv, perm, gram, base)
    recv = lax.all_to_all(pack, EVERY, 0, 0, tiled=True)
    nll, loss, norm = pl.pallas_call(
        functools.partial(final_kernel, sizes),
        in_specs=[VMEM] * 2,
        out_specs=[VMEM] * 3,
        out_shape=[shape(1, count), shape(1, 1), shape(1, 1)],
        compiler_params=params,
        name="final",
    )(recv, keep)
    return (nll, loss[0, 0], norm[0, 0])


def solution(mesh):
    placed = (
        P("depth", GROUP, None),
        P(GROUP, None),
        P("depth", GROUP),
        P("depth", GROUP),
    )
    return jax.shard_map(
        program,
        mesh=mesh,
        in_specs=placed,
        out_specs=(P("depth", GROUP), P(), P()),
        check_vma=False,
    )
```

```python
import functools

import jax
import jax.numpy as jnp
from jax import lax
from jax.experimental import pallas as pl
from jax.experimental.pallas import tpu as pltpu
from jax.sharding import PartitionSpec as P


GROUP = ("seq", "vocab")
EVERY = ("seq", "depth", "vocab")
SCALE = 2.0**40
WEIGHTS = (1.0, 0.3)
LIMIT = 24 * 2**20
PIECES = 2
LEAN = -256
VMEM = pl.BlockSpec(memory_space=pltpu.VMEM)


def exchange_masks(size):
    bits = size.bit_length() - 1
    assert size == 2**bits and bits >= 2
    return [2**bit for bit in range(bits - 1, 1, -1)] + [1, 2]


def moved(value, axis, mask):
    return lax.ppermute(value, axis, [(at, at ^ mask) for at in range(lax.axis_size(axis))])


def joined(value, other, mask):
    later = (lax.axis_index("vocab") & mask) != 0
    return jnp.concatenate([jnp.where(later, other, value), jnp.where(later, value, other)], axis=0)


def slot_of(masks):
    at = lax.axis_index("vocab")
    return sum(jnp.where((at & mask) != 0, 1, 0) << turn for turn, mask in enumerate(masks))


def rows_dot(a, b, dims):
    return lax.dot_general(a, b, ((dims[:1], dims[1:]), ((), ())), preferred_element_type=jnp.float32)


def fetch_kernel(start, table_ref, copy_ref, sems):
    pieces, columns = sems.shape[0], copy_ref.shape[1]
    chunk = columns // pieces
    copies = [
        pltpu.make_async_copy(
            table_ref.at[:, pl.ds(start + at * chunk, chunk)], copy_ref.at[:, pl.ds(at * chunk, chunk)], sems.at[at]
        )
        for at in range(pieces)
    ]
    for copy in copies:
        copy.start()
    for copy in copies:
        copy.wait()


def merged(own_ref, twin_ref):
    first = lax.axis_index("seq") == 0
    own, twin = own_ref[...], twin_ref[...]
    return jnp.concatenate([jnp.where(first, own, twin), jnp.where(first, twin, own)], axis=0)


def early_kernel(own_ref, twin_ref, table_ref, logits_ref, gram_ref, states_ref):
    states = merged(own_ref, twin_ref)
    states_ref[...] = states
    logits_ref[: table_ref.shape[0], :] = rows_dot(table_ref[...], states, (1, 1))
    gram_ref[...] = rows_dot(states, states, (1, 1))


def folded(block, which):
    tokens = block.shape[1]
    turned = pltpu.roll(block, tokens // 2, 1)
    first = jnp.where(which == 0, block, turned)
    second = jnp.where(which == 0, turned, block)
    lane = lax.broadcasted_iota(jnp.int32, (4, tokens), 1)
    return [
        jnp.where(lane < tokens // 2, first[at : at + 4], second[at + 4 : at + 8])
        for at in range(0, block.shape[0], 8)
    ]


def logits_kernel(
    width, half, size, own_ref, twin_ref, table_ref, early_ref, gram_early_ref, states_ref, side_ref, meta_ref,
    logits_ref, send_ref, gram_ref, pack_ref,
):
    early = states_ref[...]
    late = merged(own_ref, twin_ref)
    start = early.shape[1]
    logits = rows_dot(table_ref[...], late, (1, 1)) + early_ref[:width, :]
    logits_ref[:width, :] = logits
    logits_ref[width:, :] = jnp.zeros((2 * half - width, logits.shape[1]), jnp.float32)
    gram_ref[...] = gram_early_ref[...] + rows_dot(late, late, (1, 1))
    cross = rows_dot(side_ref[:, :start], early, (1, 1)) + rows_dot(side_ref[:, start:], late, (1, 1))
    depth = lax.axis_index("depth")
    send_ref[...] = logits_ref[pl.ds(pl.multiple_of((1 - depth) * half, 8), half), :]
    peak = jnp.max(logits, axis=0, keepdims=True)
    total = jnp.sum(jnp.exp(logits - peak), axis=0, keepdims=True)
    rows = lax.broadcasted_iota(jnp.int32, meta_ref.shape, 0)
    stats = jnp.where(rows == 0, peak, jnp.where(rows == 1, total, meta_ref[...]))
    parts = [stats] + folded(cross, lax.axis_index("seq") ^ depth)
    for peer in range(size):
        for at, part in enumerate(parts):
            pack_ref[peer * len(parts) + at] = part


def gradient_kernel(
    masks, width, half, sizes, logits_ref, peer_ref, recv_ref, gram_ref, base_ref, pack_ref, keep_ref
):
    cores, vocabs, count = sizes
    depth = lax.axis_index("depth")
    tokens = gram_ref.shape[0]
    stride = 1 + count // 8
    peers = [(core, at) for core in range(cores) for at in range(vocabs)]

    def first(core, which, at):
        return ((core * 2 + which) * vocabs + at) * stride

    def head(which):
        parts = [recv_ref[first(core, which, at)] for core, at in peers]
        peak = functools.reduce(jnp.maximum, parts)[0:1, :]
        total = sum(part[1:2, :] * jnp.exp(part[0:1, :] - peak) for part in parts)
        meta = functools.reduce(jnp.add, parts)
        live = meta[3:4, :]
        weight = jnp.where(which == 0, jnp.float32(WEIGHTS[0]), jnp.float32(WEIGHTS[1]))
        scale = live * (weight / jnp.maximum(jnp.sum(live), 1.0))
        return peak + jnp.log(total), meta[2:3, :], scale

    lse, target, scale = head(depth)
    lse_peer, target_peer, scale_peer = head(1 - depth)
    rows = lax.broadcasted_iota(jnp.int32, (8, tokens), 0)
    vectors = jnp.zeros((8, tokens), jnp.float32)
    for at, vector in enumerate((lse, target, scale, lse_peer, target_peer, scale_peer)):
        vectors = jnp.where(rows == at, vector, vectors)
    keep_ref[...] = vectors

    base = base_ref[0]
    shift = pl.multiple_of(depth * half, 8)

    def gradient(logits, at, start):
        row = lax.broadcasted_iota(jnp.int32, logits.shape, 0) + start
        hit = (row + base) == vectors[at + 1 : at + 2, :].astype(jnp.int32)
        soft = jnp.exp(logits - vectors[at : at + 1, :]) - jnp.where(hit, 1.0, 0.0)
        grad = (vectors[at + 2 : at + 3, :] * SCALE) * soft
        return hit & (row < width), jnp.where(row < width, grad, 0.0).astype(jnp.bfloat16)

    logits = logits_ref[...]
    hit, grad = gradient(logits, 0, 0)
    chosen = jnp.sum(jnp.where(hit, logits, 0.0), axis=0, keepdims=True)
    _, mine = gradient(logits_ref[pl.ds(shift, half), :], 0, shift)
    _, grad_peer = gradient(peer_ref[...], 3, shift)
    inner = rows_dot(grad, grad, (0, 0))
    cross = rows_dot(grad_peer, mine, (0, 0))
    square = inner * gram_ref[...]
    flat = jnp.transpose(cross)
    lines = []
    for core in range(cores):
        for matrix, which in ((cross, depth), (flat, 1 - depth)):
            start = core * vocabs * count
            blocks = folded(matrix[start : start + vocabs * count], which ^ core)
            for at in range(vocabs):
                slot = sum(1 << turn for turn, mask in enumerate(masks) if at & mask)
                for part in range(count // 8):
                    tile = recv_ref[first(core, which, at) + 1 + part]
                    lines.append(blocks[slot * (count // 8) + part] * tile)
    square = jnp.sum(square, axis=0, keepdims=True) + 2.0 * jnp.sum(sum(lines), axis=0, keepdims=True)
    pack = jnp.where(rows == depth, chosen, jnp.where(rows == 2, square, 0.0))[:4]
    for peer in range(2 * len(peers)):
        pack_ref[peer] = pack


def final_kernel(masks, sizes, recv_ref, keep_ref, nll_ref, loss_ref, norm_ref):
    _, vocabs, count = sizes
    depth = lax.axis_index("depth")
    total = jnp.sum(recv_ref[...], axis=0)
    keep = keep_ref[...]
    own = jnp.where(depth == 0, total[0:1, :], total[1:2, :])
    peer = jnp.where(depth == 0, total[1:2, :], total[0:1, :])
    nll = keep[0:1, :] - own
    parts = keep[2:3, :] * nll + keep[5:6, :] * (keep[3:4, :] - peer)
    loss_ref[...] = jnp.sum(parts, axis=1, keepdims=True)
    square = jnp.maximum(jnp.sum(total[2:3, :], axis=1, keepdims=True), 0.0)
    norm_ref[...] = jnp.sqrt(square) * (1.0 / SCALE)
    tokens = nll.shape[1]
    place = lax.axis_index("seq") * vocabs + slot_of(masks)
    turned = pltpu.roll(jnp.broadcast_to(nll, (8, tokens)), tokens - place * count, 1)
    nll_ref[...] = turned[:1, :count]


def program(hidden, embedding, targets, mask):
    cores, depths, vocabs = (lax.axis_size(axis) for axis in EVERY)
    count, dim = hidden.shape[1:]
    assert cores == 2 and depths == 2 and count % 8 == 0 and dim % 512 == 0
    width = embedding.shape[0]
    half = -(-width // 16) * 8
    tokens = cores * vocabs * count
    size = cores * depths * vocabs
    masks = exchange_masks(vocabs)
    place = lax.axis_index(GROUP)
    sizes = (cores, vocabs, count)
    f32 = jnp.float32
    split = dim // 2 + LEAN
    assert split % 256 == 0

    own = hidden[0]
    side = moved(own, "depth", 1)
    held = own
    for mask_far in masks[:-2]:
        other = moved(held, "vocab", mask_far)
        held = joined(held, other, mask_far)
    left, right = held[:, :split], held[:, split:]
    rows = left.shape[0]
    low, high = masks[-2:]
    other = moved(left, "vocab", low)
    left = joined(left, other, low)
    other = moved(right, "vocab", high)
    right = joined(right, other, high)
    left = joined(left, moved(left, "vocab", high), high)
    last = moved(right, "vocab", low)
    parts = [joined(right[at : at + rows], last[at : at + rows], low) for at in (0, rows)]
    right = jnp.concatenate(parts, axis=0)
    left_twin = moved(left, "seq", 1)
    right_twin = moved(right, "seq", 1)

    spot_at = (lax.axis_index("seq") * vocabs + slot_of(masks)) * count
    lane = lax.broadcasted_iota(jnp.int32, (count, tokens), 1)
    spot = (lane == spot_at + lax.broadcasted_iota(jnp.int32, (count, tokens), 0)).astype(f32)
    placed = [jnp.sum(spot * value[0][:, None].astype(f32), axis=0) for value in (targets, mask)]
    line = lax.broadcasted_iota(jnp.int32, (4, tokens), 0)
    meta = jnp.where(line == 2, placed[0][None, :], jnp.where(line == 3, placed[1][None, :], 0.0))

    shape = lambda *dims: jax.ShapeDtypeStruct(dims, f32)
    params = pltpu.CompilerParams(vmem_limit_bytes=LIMIT)
    tables = []
    for start, columns in ((0, split), (split, dim - split)):
        tables.append(
            pl.pallas_call(
                functools.partial(fetch_kernel, start),
                in_specs=[pl.BlockSpec(memory_space=pltpu.HBM)],
                out_specs=VMEM,
                out_shape=pltpu.VMEM((width, columns), embedding.dtype),
                scratch_shapes=[pltpu.SemaphoreType.DMA((PIECES,))],
                compiler_params=pltpu.CompilerParams(vmem_limit_bytes=46 * 2**20),
                cost_estimate=pl.CostEstimate(flops=0, transcendentals=0, bytes_accessed=4 * width * columns),
            )(embedding)
        )
    tables = [pltpu.with_memory_space_constraint(table, pltpu.VMEM) for table in tables]
    early = pl.pallas_call(
        early_kernel,
        in_specs=[VMEM] * 3,
        out_specs=[VMEM] * 3,
        out_shape=[shape(2 * half, tokens), shape(tokens, tokens), jax.ShapeDtypeStruct((tokens, split), hidden.dtype)],
        compiler_params=params,
        name="early",
    )(left, left_twin, tables[0])
    logits, send, gram, pack = pl.pallas_call(
        functools.partial(logits_kernel, width, half, size),
        in_specs=[VMEM] * 8,
        out_specs=[VMEM] * 4,
        out_shape=[
            shape(2 * half, tokens),
            shape(half, tokens),
            shape(tokens, tokens),
            shape(size * (1 + count // 8), 4, tokens),
        ],
        compiler_params=params,
        name="logits",
    )(right, right_twin, tables[1], *early, side, meta)

    peer = moved(send, "depth", 1)
    recv = lax.all_to_all(pack, EVERY, 0, 0, tiled=True)
    base = (place * width).astype(jnp.int32).reshape(1)
    pack, keep = pl.pallas_call(
        functools.partial(gradient_kernel, masks, width, half, sizes),
        in_specs=[VMEM] * 4 + [pl.BlockSpec(memory_space=pltpu.SMEM)],
        out_specs=[VMEM] * 2,
        out_shape=[shape(size, 4, tokens), shape(8, tokens)],
        compiler_params=params,
        name="gradient",
    )(logits, peer, recv, gram, base)
    recv = lax.all_to_all(pack, EVERY, 0, 0, tiled=True)
    nll, loss, norm = pl.pallas_call(
        functools.partial(final_kernel, masks, sizes),
        in_specs=[VMEM] * 2,
        out_specs=[VMEM] * 3,
        out_shape=[shape(1, count), shape(1, 1), shape(1, 1)],
        compiler_params=params,
        name="final",
    )(recv, keep)
    return (nll, loss[0, 0], norm[0, 0])


def solution(mesh):
    placed = (
        P("depth", GROUP, None),
        P(GROUP, None),
        P("depth", GROUP),
        P("depth", GROUP),
    )
    return jax.shard_map(
        program,
        mesh=mesh,
        in_specs=placed,
        out_specs=(P("depth", GROUP), P(), P()),
        check_vma=False,
    )
```

```python
import functools

import jax
import jax.numpy as jnp
from jax import lax
from jax.experimental import pallas as pl
from jax.experimental.pallas import tpu as pltpu
from jax.sharding import PartitionSpec as P


GROUP = ("seq", "vocab")
EVERY = ("seq", "depth", "vocab")
SCALE = 2.0**40
WEIGHTS = (1.0, 0.3)
LIMIT = 24 * 2**20
PIECES = 2
LEAN = -256
VMEM = pl.BlockSpec(memory_space=pltpu.VMEM)


def exchange_steps(size):
    bits = size.bit_length() - 1
    assert size == 2**bits and bits >= 3
    return [(2**bit, 2**bit) for bit in range(bits - 1, 2, -1)] + [(6, 4), (1, 1), (2, 6)]


def parity(at, bits):
    return functools.reduce(lambda x, y: x ^ y, [(at >> bit) & 1 for bit in range(bits.bit_length()) if bits >> bit & 1])


def moved(value, axis, mask):
    return lax.ppermute(value, axis, [(at, at ^ mask) for at in range(lax.axis_size(axis))])


def joined(value, other, bits):
    later = parity(lax.axis_index("vocab"), bits) != 0
    return jnp.concatenate([jnp.where(later, other, value), jnp.where(later, value, other)], axis=0)


def slot_of(steps, at):
    return sum(parity(at, bits) << turn for turn, (_, bits) in enumerate(steps))


def rows_dot(a, b, dims):
    return lax.dot_general(a, b, ((dims[:1], dims[1:]), ((), ())), preferred_element_type=jnp.float32)


def fetch_kernel(start, table_ref, copy_ref, sems):
    pieces, columns = sems.shape[0], copy_ref.shape[1]
    chunk = columns // pieces
    copies = [
        pltpu.make_async_copy(
            table_ref.at[:, pl.ds(start + at * chunk, chunk)], copy_ref.at[:, pl.ds(at * chunk, chunk)], sems.at[at]
        )
        for at in range(pieces)
    ]
    for copy in copies:
        copy.start()
    for copy in copies:
        copy.wait()


def merged(own_ref, twin_ref):
    first = lax.axis_index("seq") == 0
    own, twin = own_ref[...], twin_ref[...]
    return jnp.concatenate([jnp.where(first, own, twin), jnp.where(first, twin, own)], axis=0)


def first_kernel(cut, own_ref, twin_ref, table_ref, logits_ref):
    states = merged(own_ref.at[:, :cut], twin_ref.at[:, :cut])
    logits_ref[: table_ref.shape[0], :] = rows_dot(table_ref[:, :cut], states, (1, 1))


def second_kernel(cut, own_ref, twin_ref, table_ref, first_ref, logits_ref, states_ref):
    states = merged(own_ref, twin_ref)
    states_ref[...] = states
    width = table_ref.shape[0]
    logits_ref[:width, :] = first_ref[:width, :] + rows_dot(table_ref[:, cut:], states[:, cut:], (1, 1))


def gram_kernel(early_ref, own_ref, twin_ref, gram_ref):
    early, late = early_ref[...], merged(own_ref, twin_ref)
    gram_ref[...] = rows_dot(early, early, (1, 1)) + rows_dot(late, late, (1, 1))


def folded(block, which):
    tokens = block.shape[1]
    turned = pltpu.roll(block, tokens // 2, 1)
    first = jnp.where(which == 0, block, turned)
    second = jnp.where(which == 0, turned, block)
    lane = lax.broadcasted_iota(jnp.int32, (4, tokens), 1)
    return [
        jnp.where(lane < tokens // 2, first[at : at + 4], second[at + 4 : at + 8])
        for at in range(0, block.shape[0], 8)
    ]


def logits_kernel(
    width, half, size, own_ref, twin_ref, table_ref, early_ref, states_ref, side_ref, meta_ref,
    logits_ref, send_ref, pack_ref,
):
    early = states_ref[...]
    late = merged(own_ref, twin_ref)
    start = early.shape[1]
    logits = rows_dot(table_ref[...], late, (1, 1)) + early_ref[:width, :]
    logits_ref[:width, :] = logits
    logits_ref[width:, :] = jnp.zeros((2 * half - width, logits.shape[1]), jnp.float32)
    cross = rows_dot(side_ref[:, :start], early, (1, 1)) + rows_dot(side_ref[:, start:], late, (1, 1))
    depth = lax.axis_index("depth")
    send_ref[...] = logits_ref[pl.ds(pl.multiple_of((1 - depth) * half, 8), half), :]
    peak = jnp.max(logits, axis=0, keepdims=True)
    total = jnp.sum(jnp.exp(logits - peak), axis=0, keepdims=True)
    rows = lax.broadcasted_iota(jnp.int32, meta_ref.shape, 0)
    stats = jnp.where(rows == 0, peak, jnp.where(rows == 1, total, meta_ref[...]))
    parts = [stats] + folded(cross, lax.axis_index("seq") ^ depth)
    for peer in range(size):
        for at, part in enumerate(parts):
            pack_ref[peer * len(parts) + at] = part


def gradient_kernel(
    steps, width, half, sizes, logits_ref, peer_ref, recv_ref, gram_ref, base_ref, pack_ref, keep_ref
):
    cores, vocabs, count = sizes
    depth = lax.axis_index("depth")
    tokens = gram_ref.shape[0]
    stride = 1 + count // 8
    peers = [(core, at) for core in range(cores) for at in range(vocabs)]

    def first(core, which, at):
        return ((core * 2 + which) * vocabs + at) * stride

    def head(which):
        parts = [recv_ref[first(core, which, at)] for core, at in peers]
        peak = functools.reduce(jnp.maximum, parts)[0:1, :]
        total = sum(part[1:2, :] * jnp.exp(part[0:1, :] - peak) for part in parts)
        meta = functools.reduce(jnp.add, parts)
        live = meta[3:4, :]
        weight = jnp.where(which == 0, jnp.float32(WEIGHTS[0]), jnp.float32(WEIGHTS[1]))
        scale = live * (weight / jnp.maximum(jnp.sum(live), 1.0))
        return peak + jnp.log(total), meta[2:3, :], scale

    lse, target, scale = head(depth)
    lse_peer, target_peer, scale_peer = head(1 - depth)
    rows = lax.broadcasted_iota(jnp.int32, (8, tokens), 0)
    vectors = jnp.zeros((8, tokens), jnp.float32)
    for at, vector in enumerate((lse, target, scale, lse_peer, target_peer, scale_peer)):
        vectors = jnp.where(rows == at, vector, vectors)
    keep_ref[...] = vectors

    base = base_ref[0]
    shift = pl.multiple_of(depth * half, 8)

    def gradient(logits, at, start):
        row = lax.broadcasted_iota(jnp.int32, logits.shape, 0) + start
        hit = (row + base) == vectors[at + 1 : at + 2, :].astype(jnp.int32)
        soft = jnp.exp(logits - vectors[at : at + 1, :]) - jnp.where(hit, 1.0, 0.0)
        grad = (vectors[at + 2 : at + 3, :] * SCALE) * soft
        return hit & (row < width), jnp.where(row < width, grad, 0.0).astype(jnp.bfloat16)

    logits = logits_ref[...]
    hit, grad = gradient(logits, 0, 0)
    chosen = jnp.sum(jnp.where(hit, logits, 0.0), axis=0, keepdims=True)
    _, mine = gradient(logits_ref[pl.ds(shift, half), :], 0, shift)
    _, grad_peer = gradient(peer_ref[...], 3, shift)
    inner = rows_dot(grad, grad, (0, 0))
    cross = rows_dot(grad_peer, mine, (0, 0))
    square = inner * gram_ref[...]
    flat = jnp.transpose(cross)
    lines = []
    for core in range(cores):
        for matrix, which in ((cross, depth), (flat, 1 - depth)):
            start = core * vocabs * count
            blocks = folded(matrix[start : start + vocabs * count], which ^ core)
            for at in range(vocabs):
                slot = slot_of(steps, at)
                for part in range(count // 8):
                    tile = recv_ref[first(core, which, at) + 1 + part]
                    lines.append(blocks[slot * (count // 8) + part] * tile)
    square = jnp.sum(square, axis=0, keepdims=True) + 2.0 * jnp.sum(sum(lines), axis=0, keepdims=True)
    pack = jnp.where(rows == depth, chosen, jnp.where(rows == 2, square, 0.0))[:4]
    for peer in range(2 * len(peers)):
        pack_ref[peer] = pack


def final_kernel(steps, sizes, recv_ref, keep_ref, nll_ref, loss_ref, norm_ref):
    _, vocabs, count = sizes
    depth = lax.axis_index("depth")
    total = jnp.sum(recv_ref[...], axis=0)
    keep = keep_ref[...]
    own = jnp.where(depth == 0, total[0:1, :], total[1:2, :])
    peer = jnp.where(depth == 0, total[1:2, :], total[0:1, :])
    nll = keep[0:1, :] - own
    parts = keep[2:3, :] * nll + keep[5:6, :] * (keep[3:4, :] - peer)
    loss_ref[...] = jnp.sum(parts, axis=1, keepdims=True)
    square = jnp.maximum(jnp.sum(total[2:3, :], axis=1, keepdims=True), 0.0)
    norm_ref[...] = jnp.sqrt(square) * (1.0 / SCALE)
    tokens = nll.shape[1]
    place = lax.axis_index("seq") * vocabs + slot_of(steps, lax.axis_index("vocab"))
    turned = pltpu.roll(jnp.broadcast_to(nll, (8, tokens)), tokens - place * count, 1)
    nll_ref[...] = turned[:1, :count]


def program(hidden, embedding, targets, mask):
    cores, depths, vocabs = (lax.axis_size(axis) for axis in EVERY)
    count, dim = hidden.shape[1:]
    assert cores == 2 and depths == 2 and count % 8 == 0 and dim % 512 == 0
    width = embedding.shape[0]
    half = -(-width // 16) * 8
    tokens = cores * vocabs * count
    size = cores * depths * vocabs
    steps = exchange_steps(vocabs)
    place = lax.axis_index(GROUP)
    sizes = (cores, vocabs, count)
    f32 = jnp.float32
    split = dim // 2 + LEAN
    assert split % 256 == 0

    own = hidden[0]
    side = moved(own, "depth", 1)
    held = own
    *far, low, high = steps
    for step in far:
        other = moved(held, "vocab", step[0])
        held = joined(held, other, step[1])
    left, right = held[:, :split], held[:, split:]
    rows = left.shape[0]
    other = moved(left, "vocab", low[0])
    left = joined(left, other, low[1])
    other = moved(right, "vocab", high[0])
    right = joined(right, other, high[1])
    left = joined(left, moved(left, "vocab", high[0]), high[1])
    last = moved(right, "vocab", low[0])
    parts = [joined(right[at : at + rows], last[at : at + rows], low[1]) for at in (0, rows)]
    right = jnp.concatenate(parts, axis=0)
    left_twin = moved(left, "seq", 1)
    right_twin = moved(right, "seq", 1)

    spot_at = (lax.axis_index("seq") * vocabs + slot_of(steps, lax.axis_index("vocab"))) * count
    lane = lax.broadcasted_iota(jnp.int32, (count, tokens), 1)
    spot = (lane == spot_at + lax.broadcasted_iota(jnp.int32, (count, tokens), 0)).astype(f32)
    placed = [jnp.sum(spot * value[0][:, None].astype(f32), axis=0) for value in (targets, mask)]
    line = lax.broadcasted_iota(jnp.int32, (4, tokens), 0)
    meta = jnp.where(line == 2, placed[0][None, :], jnp.where(line == 3, placed[1][None, :], 0.0))

    shape = lambda *dims: jax.ShapeDtypeStruct(dims, f32)
    params = pltpu.CompilerParams(vmem_limit_bytes=LIMIT)
    tables = []
    for start, columns in ((0, split), (split, dim - split)):
        tables.append(
            pl.pallas_call(
                functools.partial(fetch_kernel, start),
                in_specs=[pl.BlockSpec(memory_space=pltpu.HBM)],
                out_specs=VMEM,
                out_shape=pltpu.VMEM((width, columns), embedding.dtype),
                scratch_shapes=[pltpu.SemaphoreType.DMA((PIECES,))],
                compiler_params=pltpu.CompilerParams(vmem_limit_bytes=4 * 2**20),
                cost_estimate=pl.CostEstimate(flops=0, transcendentals=0, bytes_accessed=4 * width * columns),
            )(pltpu.with_memory_space_constraint(embedding, pltpu.HBM))
        )
    tables = [pltpu.with_memory_space_constraint(table, pltpu.VMEM) for table in tables]
    cut = split // 2
    first = pl.pallas_call(
        functools.partial(first_kernel, cut),
        in_specs=[VMEM] * 3,
        out_specs=VMEM,
        out_shape=shape(2 * half, tokens),
        compiler_params=params,
        name="first",
    )(left, left_twin, tables[0])
    early, states = pl.pallas_call(
        functools.partial(second_kernel, cut),
        in_specs=[VMEM] * 4,
        out_specs=[VMEM] * 2,
        out_shape=[shape(2 * half, tokens), jax.ShapeDtypeStruct((tokens, split), hidden.dtype)],
        compiler_params=params,
        name="second",
    )(left, left_twin, tables[0], first)
    logits, send, pack = pl.pallas_call(
        functools.partial(logits_kernel, width, half, size),
        in_specs=[VMEM] * 7,
        out_specs=[VMEM] * 3,
        out_shape=[
            shape(2 * half, tokens),
            shape(half, tokens),
            shape(size * (1 + count // 8), 4, tokens),
        ],
        compiler_params=params,
        name="logits",
    )(right, right_twin, tables[1], early, states, side, meta)

    peer = moved(send, "depth", 1)
    recv = lax.all_to_all(pack, EVERY, 0, 0, tiled=True)
    gram = pl.pallas_call(
        gram_kernel,
        in_specs=[VMEM] * 3,
        out_specs=VMEM,
        out_shape=shape(tokens, tokens),
        compiler_params=params,
        name="gram",
    )(states, right, right_twin)
    base = (place * width).astype(jnp.int32).reshape(1)
    pack, keep = pl.pallas_call(
        functools.partial(gradient_kernel, steps, width, half, sizes),
        in_specs=[VMEM] * 4 + [pl.BlockSpec(memory_space=pltpu.SMEM)],
        out_specs=[VMEM] * 2,
        out_shape=[shape(size, 4, tokens), shape(8, tokens)],
        compiler_params=params,
        name="gradient",
    )(logits, peer, recv, gram, base)
    recv = lax.all_to_all(pack, EVERY, 0, 0, tiled=True)
    nll, loss, norm = pl.pallas_call(
        functools.partial(final_kernel, steps, sizes),
        in_specs=[VMEM] * 2,
        out_specs=[VMEM] * 3,
        out_shape=[shape(1, count), shape(1, 1), shape(1, 1)],
        compiler_params=params,
        name="final",
    )(recv, keep)
    return (nll, loss[0, 0], norm[0, 0])


def solution(mesh):
    placed = (
        P("depth", GROUP, None),
        P(GROUP, None),
        P("depth", GROUP),
        P("depth", GROUP),
    )
    return jax.shard_map(
        program,
        mesh=mesh,
        in_specs=placed,
        out_specs=(P("depth", GROUP), P(), P()),
        check_vma=False,
    )
```

```python
import functools

import jax
import jax.numpy as jnp
from jax import lax
from jax.experimental import pallas as pl
from jax.experimental.pallas import tpu as pltpu
from jax.sharding import PartitionSpec as P


GROUP = ("seq", "vocab")
EVERY = ("seq", "depth", "vocab")
SCALE = 2.0**40
WEIGHTS = (1.0, 0.3)
LIMIT = 24 * 2**20
PIECES = 1
LEAN = 256
VMEM = pl.BlockSpec(memory_space=pltpu.VMEM)


def exchange_steps(size):
    bits = size.bit_length() - 1
    assert size == 2**bits and bits >= 3
    return [(2**bit, 2**bit) for bit in range(bits - 1, 2, -1)] + [(6, 4), (1, 1), (2, 6)]


def parity(at, bits):
    return functools.reduce(lambda x, y: x ^ y, [(at >> bit) & 1 for bit in range(bits.bit_length()) if bits >> bit & 1])


def moved(value, axis, mask):
    return lax.ppermute(value, axis, [(at, at ^ mask) for at in range(lax.axis_size(axis))])


def joined(value, other, bits):
    later = parity(lax.axis_index("vocab"), bits) != 0
    return jnp.concatenate([jnp.where(later, other, value), jnp.where(later, value, other)], axis=0)


def slot_of(steps, at):
    return sum(parity(at, bits) << turn for turn, (_, bits) in enumerate(steps))


def rows_dot(a, b, dims):
    return lax.dot_general(a, b, ((dims[:1], dims[1:]), ((), ())), preferred_element_type=jnp.float32)


def fetch_kernel(start, table_ref, copy_ref, sems):
    pieces, columns = sems.shape[0], copy_ref.shape[1]
    chunk = columns // pieces
    copies = [
        pltpu.make_async_copy(
            table_ref.at[:, pl.ds(start + at * chunk, chunk)], copy_ref.at[:, pl.ds(at * chunk, chunk)], sems.at[at]
        )
        for at in range(pieces)
    ]
    for copy in copies:
        copy.start()
    for copy in copies:
        copy.wait()


def merged(own_ref, twin_ref):
    first = lax.axis_index("seq") == 0
    own, twin = own_ref[...], twin_ref[...]
    return jnp.concatenate([jnp.where(first, own, twin), jnp.where(first, twin, own)], axis=0)


def first_kernel(cut, own_ref, twin_ref, table_ref, logits_ref):
    states = merged(own_ref.at[:, :cut], twin_ref.at[:, :cut])
    logits_ref[: table_ref.shape[0], :] = rows_dot(table_ref[...], states, (1, 1))


def second_kernel(cut, own_ref, twin_ref, table_ref, first_ref, logits_ref, states_ref):
    states = merged(own_ref, twin_ref)
    states_ref[...] = states
    width = table_ref.shape[0]
    logits_ref[:width, :] = first_ref[:width, :] + rows_dot(table_ref[...], states[:, cut:], (1, 1))


def gram_kernel(early_ref, own_ref, twin_ref, gram_ref):
    early, late = early_ref[...], merged(own_ref, twin_ref)
    gram_ref[...] = rows_dot(early, early, (1, 1)) + rows_dot(late, late, (1, 1))


def folded(block, which):
    tokens = block.shape[1]
    turned = pltpu.roll(block, tokens // 2, 1)
    first = jnp.where(which == 0, block, turned)
    second = jnp.where(which == 0, turned, block)
    lane = lax.broadcasted_iota(jnp.int32, (4, tokens), 1)
    return [
        jnp.where(lane < tokens // 2, first[at : at + 4], second[at + 4 : at + 8])
        for at in range(0, block.shape[0], 8)
    ]


def logits_kernel(
    width, half, size, own_ref, twin_ref, table_ref, early_ref, states_ref, side_ref, meta_ref,
    logits_ref, send_ref, pack_ref,
):
    early = states_ref[...]
    late = merged(own_ref, twin_ref)
    start = early.shape[1]
    logits = rows_dot(table_ref[...], late, (1, 1)) + early_ref[:width, :]
    logits_ref[:width, :] = logits
    logits_ref[width:, :] = jnp.zeros((2 * half - width, logits.shape[1]), jnp.float32)
    cross = rows_dot(side_ref[:, :start], early, (1, 1)) + rows_dot(side_ref[:, start:], late, (1, 1))
    depth = lax.axis_index("depth")
    send_ref[...] = logits_ref[pl.ds(pl.multiple_of((1 - depth) * half, 8), half), :]
    peak = jnp.max(logits, axis=0, keepdims=True)
    total = jnp.sum(jnp.exp(logits - peak), axis=0, keepdims=True)
    rows = lax.broadcasted_iota(jnp.int32, meta_ref.shape, 0)
    stats = jnp.where(rows == 0, peak, jnp.where(rows == 1, total, meta_ref[...]))
    parts = [stats] + folded(cross, lax.axis_index("seq") ^ depth)
    for peer in range(size):
        for at, part in enumerate(parts):
            pack_ref[peer * len(parts) + at] = part


def gradient_kernel(
    steps, width, half, sizes, logits_ref, peer_ref, recv_ref, gram_ref, base_ref, pack_ref, keep_ref
):
    cores, vocabs, count = sizes
    depth = lax.axis_index("depth")
    tokens = gram_ref.shape[0]
    stride = 1 + count // 8
    peers = [(core, at) for core in range(cores) for at in range(vocabs)]

    def first(core, which, at):
        return ((core * 2 + which) * vocabs + at) * stride

    def head(which):
        parts = [recv_ref[first(core, which, at)] for core, at in peers]
        peak = functools.reduce(jnp.maximum, parts)[0:1, :]
        total = sum(part[1:2, :] * jnp.exp(part[0:1, :] - peak) for part in parts)
        meta = functools.reduce(jnp.add, parts)
        live = meta[3:4, :]
        weight = jnp.where(which == 0, jnp.float32(WEIGHTS[0]), jnp.float32(WEIGHTS[1]))
        scale = live * (weight / jnp.maximum(jnp.sum(live), 1.0))
        return peak + jnp.log(total), meta[2:3, :], scale

    lse, target, scale = head(depth)
    lse_peer, target_peer, scale_peer = head(1 - depth)
    rows = lax.broadcasted_iota(jnp.int32, (8, tokens), 0)
    vectors = jnp.zeros((8, tokens), jnp.float32)
    for at, vector in enumerate((lse, target, scale, lse_peer, target_peer, scale_peer)):
        vectors = jnp.where(rows == at, vector, vectors)
    keep_ref[...] = vectors

    base = base_ref[0]
    shift = pl.multiple_of(depth * half, 8)

    def gradient(logits, at, start):
        row = lax.broadcasted_iota(jnp.int32, logits.shape, 0) + start
        hit = (row + base) == vectors[at + 1 : at + 2, :].astype(jnp.int32)
        soft = jnp.exp(logits - vectors[at : at + 1, :]) - jnp.where(hit, 1.0, 0.0)
        grad = (vectors[at + 2 : at + 3, :] * SCALE) * soft
        return hit & (row < width), jnp.where(row < width, grad, 0.0).astype(jnp.bfloat16)

    logits = logits_ref[...]
    hit, grad = gradient(logits, 0, 0)
    chosen = jnp.sum(jnp.where(hit, logits, 0.0), axis=0, keepdims=True)
    _, mine = gradient(logits_ref[pl.ds(shift, half), :], 0, shift)
    _, grad_peer = gradient(peer_ref[...], 3, shift)
    inner = rows_dot(grad, grad, (0, 0))
    cross = rows_dot(grad_peer, mine, (0, 0))
    square = inner * gram_ref[...]
    flat = jnp.transpose(cross)
    lines = []
    for core in range(cores):
        for matrix, which in ((cross, depth), (flat, 1 - depth)):
            start = core * vocabs * count
            blocks = folded(matrix[start : start + vocabs * count], which ^ core)
            for at in range(vocabs):
                slot = slot_of(steps, at)
                for part in range(count // 8):
                    tile = recv_ref[first(core, which, at) + 1 + part]
                    lines.append(blocks[slot * (count // 8) + part] * tile)
    square = jnp.sum(square, axis=0, keepdims=True) + 2.0 * jnp.sum(sum(lines), axis=0, keepdims=True)
    pack = jnp.where(rows == depth, chosen, jnp.where(rows == 2, square, 0.0))[:4]
    for peer in range(2 * len(peers)):
        pack_ref[peer] = pack


def final_kernel(steps, sizes, recv_ref, keep_ref, nll_ref, loss_ref, norm_ref):
    _, vocabs, count = sizes
    depth = lax.axis_index("depth")
    total = jnp.sum(recv_ref[...], axis=0)
    keep = keep_ref[...]
    own = jnp.where(depth == 0, total[0:1, :], total[1:2, :])
    peer = jnp.where(depth == 0, total[1:2, :], total[0:1, :])
    nll = keep[0:1, :] - own
    parts = keep[2:3, :] * nll + keep[5:6, :] * (keep[3:4, :] - peer)
    loss_ref[...] = jnp.sum(parts, axis=1, keepdims=True)
    square = jnp.maximum(jnp.sum(total[2:3, :], axis=1, keepdims=True), 0.0)
    norm_ref[...] = jnp.sqrt(square) * (1.0 / SCALE)
    tokens = nll.shape[1]
    place = lax.axis_index("seq") * vocabs + slot_of(steps, lax.axis_index("vocab"))
    turned = pltpu.roll(jnp.broadcast_to(nll, (8, tokens)), tokens - place * count, 1)
    nll_ref[...] = turned[:1, :count]


def program(hidden, embedding, targets, mask):
    cores, depths, vocabs = (lax.axis_size(axis) for axis in EVERY)
    count, dim = hidden.shape[1:]
    assert cores == 2 and depths == 2 and count % 8 == 0 and dim % 512 == 0
    width = embedding.shape[0]
    half = -(-width // 16) * 8
    tokens = cores * vocabs * count
    size = cores * depths * vocabs
    steps = exchange_steps(vocabs)
    place = lax.axis_index(GROUP)
    sizes = (cores, vocabs, count)
    f32 = jnp.float32
    split = dim // 2 + LEAN
    assert split % 256 == 0

    own = hidden[0]
    side = moved(own, "depth", 1)
    held = own
    *far, low, high = steps
    for step in far:
        other = moved(held, "vocab", step[0])
        held = joined(held, other, step[1])
    left, right = held[:, :split], held[:, split:]
    rows = left.shape[0]
    other = moved(left, "vocab", low[0])
    left = joined(left, other, low[1])
    other = moved(right, "vocab", high[0])
    right = joined(right, other, high[1])
    left = joined(left, moved(left, "vocab", high[0]), high[1])
    last = moved(right, "vocab", low[0])
    parts = [joined(right[at : at + rows], last[at : at + rows], low[1]) for at in (0, rows)]
    right = jnp.concatenate(parts, axis=0)
    left_twin = moved(left, "seq", 1)
    right_twin = moved(right, "seq", 1)

    spot_at = (lax.axis_index("seq") * vocabs + slot_of(steps, lax.axis_index("vocab"))) * count
    lane = lax.broadcasted_iota(jnp.int32, (count, tokens), 1)
    spot = (lane == spot_at + lax.broadcasted_iota(jnp.int32, (count, tokens), 0)).astype(f32)
    placed = [jnp.sum(spot * value[0][:, None].astype(f32), axis=0) for value in (targets, mask)]
    line = lax.broadcasted_iota(jnp.int32, (4, tokens), 0)
    meta = jnp.where(line == 2, placed[0][None, :], jnp.where(line == 3, placed[1][None, :], 0.0))

    shape = lambda *dims: jax.ShapeDtypeStruct(dims, f32)
    params = pltpu.CompilerParams(vmem_limit_bytes=LIMIT)
    cut = split // 2
    fetches = ((0, cut), (cut, cut), (split, dim - split))
    tables = []
    for start, columns in fetches:
        tables.append(
            pl.pallas_call(
                functools.partial(fetch_kernel, start),
                in_specs=[pl.BlockSpec(memory_space=pltpu.HBM)],
                out_specs=VMEM,
                out_shape=pltpu.VMEM((width, columns), embedding.dtype),
                scratch_shapes=[pltpu.SemaphoreType.DMA((PIECES,))],
                compiler_params=pltpu.CompilerParams(vmem_limit_bytes=4 * 2**20),
                cost_estimate=pl.CostEstimate(flops=0, transcendentals=0, bytes_accessed=4 * width * columns),
            )(pltpu.with_memory_space_constraint(embedding, pltpu.HBM))
        )
    tables = [pltpu.with_memory_space_constraint(table, pltpu.VMEM) for table in tables]
    first = pl.pallas_call(
        functools.partial(first_kernel, cut),
        in_specs=[VMEM] * 3,
        out_specs=VMEM,
        out_shape=shape(2 * half, tokens),
        compiler_params=params,
        name="first",
    )(left, left_twin, tables[0])
    early, states = pl.pallas_call(
        functools.partial(second_kernel, cut),
        in_specs=[VMEM] * 4,
        out_specs=[VMEM] * 2,
        out_shape=[shape(2 * half, tokens), jax.ShapeDtypeStruct((tokens, split), hidden.dtype)],
        compiler_params=params,
        name="second",
    )(left, left_twin, tables[1], first)
    logits, send, pack = pl.pallas_call(
        functools.partial(logits_kernel, width, half, size),
        in_specs=[VMEM] * 7,
        out_specs=[VMEM] * 3,
        out_shape=[
            shape(2 * half, tokens),
            shape(half, tokens),
            shape(size * (1 + count // 8), 4, tokens),
        ],
        compiler_params=params,
        name="logits",
    )(right, right_twin, tables[2], early, states, side, meta)

    peer = moved(send, "depth", 1)
    recv = lax.all_to_all(pack, EVERY, 0, 0, tiled=True)
    gram = pl.pallas_call(
        gram_kernel,
        in_specs=[VMEM] * 3,
        out_specs=VMEM,
        out_shape=shape(tokens, tokens),
        compiler_params=params,
        name="gram",
    )(states, right, right_twin)
    base = (place * width).astype(jnp.int32).reshape(1)
    pack, keep = pl.pallas_call(
        functools.partial(gradient_kernel, steps, width, half, sizes),
        in_specs=[VMEM] * 4 + [pl.BlockSpec(memory_space=pltpu.SMEM)],
        out_specs=[VMEM] * 2,
        out_shape=[shape(size, 4, tokens), shape(8, tokens)],
        compiler_params=params,
        name="gradient",
    )(logits, peer, recv, gram, base)
    recv = lax.all_to_all(pack, EVERY, 0, 0, tiled=True)
    nll, loss, norm = pl.pallas_call(
        functools.partial(final_kernel, steps, sizes),
        in_specs=[VMEM] * 2,
        out_specs=[VMEM] * 3,
        out_shape=[shape(1, count), shape(1, 1), shape(1, 1)],
        compiler_params=params,
        name="final",
    )(recv, keep)
    return (nll, loss[0, 0], norm[0, 0])


def solution(mesh):
    placed = (
        P("depth", GROUP, None),
        P(GROUP, None),
        P("depth", GROUP),
        P("depth", GROUP),
    )
    return jax.shard_map(
        program,
        mesh=mesh,
        in_specs=placed,
        out_specs=(P("depth", GROUP), P(), P()),
        check_vma=False,
    )
```

```python
import functools

import jax
import jax.numpy as jnp
from jax import lax
from jax.experimental import pallas as pl
from jax.experimental.pallas import tpu as pltpu
from jax.sharding import PartitionSpec as P


GROUP = ("seq", "vocab")
EVERY = ("seq", "depth", "vocab")
SCALE = 2.0**40
WEIGHTS = (1.0, 0.3)
LIMIT = 24 * 2**20
PIECES = 2
LEAN = -256
VMEM = pl.BlockSpec(memory_space=pltpu.VMEM)


def exchange_steps(size):
    bits = size.bit_length() - 1
    assert size == 2**bits and bits >= 3
    return [(2**bit, 2**bit) for bit in range(bits - 1, 2, -1)] + [(6, 4), (1, 1), (2, 6)]


def parity(at, bits):
    return functools.reduce(lambda x, y: x ^ y, [(at >> bit) & 1 for bit in range(bits.bit_length()) if bits >> bit & 1])


def moved(value, axis, mask):
    return lax.ppermute(value, axis, [(at, at ^ mask) for at in range(lax.axis_size(axis))])


def joined(value, other, bits):
    later = parity(lax.axis_index("vocab"), bits) != 0
    return jnp.concatenate([jnp.where(later, other, value), jnp.where(later, value, other)], axis=0)


def slot_of(steps, at):
    return sum(parity(at, bits) << turn for turn, (_, bits) in enumerate(steps))


def rows_dot(a, b, dims):
    return lax.dot_general(a, b, ((dims[:1], dims[1:]), ((), ())), preferred_element_type=jnp.float32)


def fetch_kernel(start, table_ref, copy_ref, sems):
    pieces, columns = sems.shape[0], copy_ref.shape[1]
    chunk = columns // pieces
    copies = [
        pltpu.make_async_copy(
            table_ref.at[:, pl.ds(start + at * chunk, chunk)], copy_ref.at[:, pl.ds(at * chunk, chunk)], sems.at[at]
        )
        for at in range(pieces)
    ]
    for copy in copies:
        copy.start()
    for copy in copies:
        copy.wait()


def merged(own_ref, twin_ref):
    first = lax.axis_index("seq") == 0
    own, twin = own_ref[...], twin_ref[...]
    return jnp.concatenate([jnp.where(first, own, twin), jnp.where(first, twin, own)], axis=0)


def first_kernel(cut, own_ref, twin_ref, table_ref, logits_ref):
    states = merged(own_ref.at[:, :cut], twin_ref.at[:, :cut])
    logits_ref[: table_ref.shape[0], :] = rows_dot(table_ref[:, :cut], states, (1, 1))


def second_kernel(cut, own_ref, twin_ref, table_ref, first_ref, logits_ref, states_ref):
    states = merged(own_ref, twin_ref)
    states_ref[...] = states
    width = table_ref.shape[0]
    logits_ref[:width, :] = first_ref[:width, :] + rows_dot(table_ref[:, cut:], states[:, cut:], (1, 1))


def gram_kernel(early_ref, own_ref, twin_ref, gram_ref):
    early, late = early_ref[...], merged(own_ref, twin_ref)
    gram_ref[...] = rows_dot(early, early, (1, 1)) + rows_dot(late, late, (1, 1))


def folded(block, which):
    tokens = block.shape[1]
    turned = pltpu.roll(block, tokens // 2, 1)
    first = jnp.where(which == 0, block, turned)
    second = jnp.where(which == 0, turned, block)
    lane = lax.broadcasted_iota(jnp.int32, (4, tokens), 1)
    return [
        jnp.where(lane < tokens // 2, first[at : at + 4], second[at + 4 : at + 8])
        for at in range(0, block.shape[0], 8)
    ]


def logits_kernel(
    width, half, size, own_ref, twin_ref, table_ref, early_ref, states_ref, side_ref, meta_ref,
    logits_ref, send_ref, pack_ref,
):
    early = states_ref[...]
    late = merged(own_ref, twin_ref)
    start = early.shape[1]
    logits = rows_dot(table_ref[...], late, (1, 1)) + early_ref[:width, :]
    logits_ref[:width, :] = logits
    logits_ref[width:, :] = jnp.zeros((2 * half - width, logits.shape[1]), jnp.float32)
    cross = rows_dot(side_ref[:, :start], early, (1, 1)) + rows_dot(side_ref[:, start:], late, (1, 1))
    depth = lax.axis_index("depth")
    send_ref[...] = logits_ref[pl.ds(pl.multiple_of((1 - depth) * half, 8), half), :]
    peak = jnp.max(logits, axis=0, keepdims=True)
    total = jnp.sum(jnp.exp(logits - peak), axis=0, keepdims=True)
    rows = lax.broadcasted_iota(jnp.int32, meta_ref.shape, 0)
    stats = jnp.where(rows == 0, peak, jnp.where(rows == 1, total, meta_ref[...]))
    parts = [stats] + folded(cross, lax.axis_index("seq") ^ depth)
    for peer in range(size):
        for at, part in enumerate(parts):
            pack_ref[peer * len(parts) + at] = part


def gradient_kernel(
    steps, width, half, sizes, logits_ref, peer_ref, recv_ref, gram_ref, pack_ref, keep_ref
):
    cores, vocabs, count = sizes
    depth = lax.axis_index("depth")
    tokens = gram_ref.shape[0]
    stride = 1 + count // 8
    peers = [(core, at) for core in range(cores) for at in range(vocabs)]

    def first(core, which, at):
        return ((core * 2 + which) * vocabs + at) * stride

    def head(which):
        parts = [recv_ref[first(core, which, at)] for core, at in peers]
        peak = functools.reduce(jnp.maximum, parts)[0:1, :]
        total = sum(part[1:2, :] * jnp.exp(part[0:1, :] - peak) for part in parts)
        meta = functools.reduce(jnp.add, parts)
        live = meta[3:4, :]
        weight = jnp.where(which == 0, jnp.float32(WEIGHTS[0]), jnp.float32(WEIGHTS[1]))
        scale = live * (weight / jnp.maximum(jnp.sum(live), 1.0))
        return peak + jnp.log(total), meta[2:3, :], scale

    lse, target, scale = head(depth)
    lse_peer, target_peer, scale_peer = head(1 - depth)
    rows = lax.broadcasted_iota(jnp.int32, (8, tokens), 0)
    vectors = jnp.zeros((8, tokens), jnp.float32)
    for at, vector in enumerate((lse, target, scale, lse_peer, target_peer, scale_peer)):
        vectors = jnp.where(rows == at, vector, vectors)
    keep_ref[...] = vectors

    base = (lax.axis_index("seq") * vocabs + lax.axis_index("vocab")) * width
    shift = pl.multiple_of(depth * half, 8)

    def gradient(logits, at, start):
        row = lax.broadcasted_iota(jnp.int32, logits.shape, 0) + start
        hit = (row + base) == vectors[at + 1 : at + 2, :].astype(jnp.int32)
        soft = jnp.exp(logits - vectors[at : at + 1, :]) - jnp.where(hit, 1.0, 0.0)
        grad = (vectors[at + 2 : at + 3, :] * SCALE) * soft
        return hit & (row < width), jnp.where(row < width, grad, 0.0).astype(jnp.bfloat16)

    logits = logits_ref[...]
    hit, grad = gradient(logits, 0, 0)
    chosen = jnp.sum(jnp.where(hit, logits, 0.0), axis=0, keepdims=True)
    _, mine = gradient(logits_ref[pl.ds(shift, half), :], 0, shift)
    _, grad_peer = gradient(peer_ref[...], 3, shift)
    inner = rows_dot(grad, grad, (0, 0))
    cross = rows_dot(grad_peer, mine, (0, 0))
    square = inner * gram_ref[...]
    flat = jnp.transpose(cross)
    lines = []
    for core in range(cores):
        for matrix, which in ((cross, depth), (flat, 1 - depth)):
            start = core * vocabs * count
            blocks = folded(matrix[start : start + vocabs * count], which ^ core)
            for at in range(vocabs):
                slot = slot_of(steps, at)
                for part in range(count // 8):
                    tile = recv_ref[first(core, which, at) + 1 + part]
                    lines.append(blocks[slot * (count // 8) + part] * tile)
    square = jnp.sum(square, axis=0, keepdims=True) + 2.0 * jnp.sum(sum(lines), axis=0, keepdims=True)
    pack = jnp.where(rows == depth, chosen, jnp.where(rows == 2, square, 0.0))[:4]
    for peer in range(2 * len(peers)):
        pack_ref[peer] = pack


def final_kernel(steps, sizes, recv_ref, keep_ref, nll_ref, loss_ref, norm_ref):
    _, vocabs, count = sizes
    depth = lax.axis_index("depth")
    total = jnp.sum(recv_ref[...], axis=0)
    keep = keep_ref[...]
    own = jnp.where(depth == 0, total[0:1, :], total[1:2, :])
    peer = jnp.where(depth == 0, total[1:2, :], total[0:1, :])
    nll = keep[0:1, :] - own
    parts = keep[2:3, :] * nll + keep[5:6, :] * (keep[3:4, :] - peer)
    loss_ref[...] = jnp.sum(parts, axis=1, keepdims=True)
    square = jnp.maximum(jnp.sum(total[2:3, :], axis=1, keepdims=True), 0.0)
    norm_ref[...] = jnp.sqrt(square) * (1.0 / SCALE)
    tokens = nll.shape[1]
    place = lax.axis_index("seq") * vocabs + slot_of(steps, lax.axis_index("vocab"))
    turned = pltpu.roll(jnp.broadcast_to(nll, (8, tokens)), tokens - place * count, 1)
    nll_ref[...] = turned[:1, :count]


def program(hidden, embedding, targets, mask):
    cores, depths, vocabs = (lax.axis_size(axis) for axis in EVERY)
    count, dim = hidden.shape[1:]
    assert cores == 2 and depths == 2 and count % 8 == 0 and dim % 512 == 0
    width = embedding.shape[0]
    half = -(-width // 16) * 8
    tokens = cores * vocabs * count
    size = cores * depths * vocabs
    steps = exchange_steps(vocabs)
    sizes = (cores, vocabs, count)
    f32 = jnp.float32
    split = dim // 2 + LEAN
    assert split % 256 == 0

    own = hidden[0]
    side = moved(own, "depth", 1)
    held = own
    *far, low, high = steps
    for step in far:
        other = moved(held, "vocab", step[0])
        held = joined(held, other, step[1])
    left, right = held[:, :split], held[:, split:]
    rows = left.shape[0]
    other = moved(left, "vocab", low[0])
    left = joined(left, other, low[1])
    other = moved(right, "vocab", high[0])
    right = joined(right, other, high[1])
    left = joined(left, moved(left, "vocab", high[0]), high[1])
    last = moved(right, "vocab", low[0])
    parts = [joined(right[at : at + rows], last[at : at + rows], low[1]) for at in (0, rows)]
    right = jnp.concatenate(parts, axis=0)
    left_twin = moved(left, "seq", 1)
    right_twin = moved(right, "seq", 1)

    spot_at = (lax.axis_index("seq") * vocabs + slot_of(steps, lax.axis_index("vocab"))) * count
    lane = lax.broadcasted_iota(jnp.int32, (count, tokens), 1)
    spot = (lane == spot_at + lax.broadcasted_iota(jnp.int32, (count, tokens), 0)).astype(f32)
    placed = [jnp.sum(spot * value[0][:, None].astype(f32), axis=0) for value in (targets, mask)]
    line = lax.broadcasted_iota(jnp.int32, (4, tokens), 0)
    meta = jnp.where(line == 2, placed[0][None, :], jnp.where(line == 3, placed[1][None, :], 0.0))

    shape = lambda *dims: jax.ShapeDtypeStruct(dims, f32)
    params = pltpu.CompilerParams(vmem_limit_bytes=LIMIT)
    tables = []
    for start, columns in ((0, split), (split, dim - split)):
        tables.append(
            pl.pallas_call(
                functools.partial(fetch_kernel, start),
                in_specs=[pl.BlockSpec(memory_space=pltpu.HBM)],
                out_specs=VMEM,
                out_shape=pltpu.VMEM((width, columns), embedding.dtype),
                scratch_shapes=[pltpu.SemaphoreType.DMA((PIECES,))],
                compiler_params=pltpu.CompilerParams(vmem_limit_bytes=4 * 2**20),
                cost_estimate=pl.CostEstimate(flops=0, transcendentals=0, bytes_accessed=4 * width * columns),
            )(pltpu.with_memory_space_constraint(embedding, pltpu.HBM))
        )
    tables = [pltpu.with_memory_space_constraint(table, pltpu.VMEM) for table in tables]
    cut = split // 2
    first = pl.pallas_call(
        functools.partial(first_kernel, cut),
        in_specs=[VMEM] * 3,
        out_specs=VMEM,
        out_shape=shape(2 * half, tokens),
        compiler_params=params,
        name="first",
    )(left, left_twin, tables[0])
    early, states = pl.pallas_call(
        functools.partial(second_kernel, cut),
        in_specs=[VMEM] * 4,
        out_specs=[VMEM] * 2,
        out_shape=[shape(2 * half, tokens), jax.ShapeDtypeStruct((tokens, split), hidden.dtype)],
        compiler_params=params,
        name="second",
    )(left, left_twin, tables[0], first)
    logits, send, pack = pl.pallas_call(
        functools.partial(logits_kernel, width, half, size),
        in_specs=[VMEM] * 7,
        out_specs=[VMEM] * 3,
        out_shape=[
            shape(2 * half, tokens),
            shape(half, tokens),
            shape(size * (1 + count // 8), 4, tokens),
        ],
        compiler_params=params,
        name="logits",
    )(right, right_twin, tables[1], early, states, side, meta)

    peer = moved(send, "depth", 1)
    recv = lax.all_to_all(pack, EVERY, 0, 0, tiled=True)
    gram = pl.pallas_call(
        gram_kernel,
        in_specs=[VMEM] * 3,
        out_specs=VMEM,
        out_shape=shape(tokens, tokens),
        compiler_params=params,
        name="gram",
    )(states, right, right_twin)
    pack, keep = pl.pallas_call(
        functools.partial(gradient_kernel, steps, width, half, sizes),
        in_specs=[VMEM] * 4,
        out_specs=[VMEM] * 2,
        out_shape=[shape(size, 4, tokens), shape(8, tokens)],
        compiler_params=params,
        name="gradient",
    )(logits, peer, recv, gram)
    recv = lax.all_to_all(pack, EVERY, 0, 0, tiled=True)
    nll, loss, norm = pl.pallas_call(
        functools.partial(final_kernel, steps, sizes),
        in_specs=[VMEM] * 2,
        out_specs=[VMEM] * 3,
        out_shape=[shape(1, count), shape(1, 1), shape(1, 1)],
        compiler_params=params,
        name="final",
    )(recv, keep)
    return (nll, loss[0, 0], norm[0, 0])


def solution(mesh):
    placed = (
        P("depth", GROUP, None),
        P(GROUP, None),
        P("depth", GROUP),
        P("depth", GROUP),
    )
    return jax.shard_map(
        program,
        mesh=mesh,
        in_specs=placed,
        out_specs=(P("depth", GROUP), P(), P()),
        check_vma=False,
    )
```
